32 devices in a mesh: dp: 8 (over y, x, core), seq: 4 (over z).
Axes of the slice: x: 2, y: 2, z: 4, core: 2. Of those that a mesh axis runs over, the one named last changes fastest.
Arguments:
- tokens: bfloat16 [32, 512, 768], P('dp', 'seq'), may hold values from -6 to 6
- cotangent: bfloat16 [32, 512, 768], P('dp', 'seq'), may hold values from -6 to 6
- lengths: int32 [32], P('dp'), may hold values from 64 to 512, as said below
- qkv_weight: bfloat16 [1, 768, 2304], P(None, ('dp', 'seq')), may hold values from -0.21875 to 0.21875
- qv_bias: bfloat16 [1, 1536], P(None, ('dp', 'seq')), may hold values from -3 to 3
- out_weight: bfloat16 [1, 768, 768], P(None, ('dp', 'seq')), may hold values from -1.75 to 1.75
- out_bias: bfloat16 [1, 768], P(None, ('dp', 'seq')), may hold values from -3 to 3
- norm_gain: bfloat16 [1, 768], P(None, ('dp', 'seq')), may hold values from 0.5 to 1.5
- norm_shift: bfloat16 [1, 768], P(None, ('dp', 'seq')), may hold values from -3 to 3
- up_weight: bfloat16 [1, 768, 3072], P(None, ('dp', 'seq')), may hold values from -0.21875 to 0.21875
- up_bias: bfloat16 [1, 3072], P(None, ('dp', 'seq')), may hold values from -3 to 3
- down_weight: bfloat16 [1, 3072, 768], P(None, ('dp', 'seq')), may hold values from -0.109375 to 0.109375
- down_bias: bfloat16 [1, 768], P(None, ('dp', 'seq')), may hold values from -3 to 3
- final_gain: bfloat16 [1, 768], P(None, ('dp', 'seq')), may hold values from 0.5 to 1.5
- final_shift: bfloat16 [1, 768], P(None, ('dp', 'seq')), may hold values from -3 to 3
Outputs:
- result: bfloat16 [32, 512, 768], P('dp', 'seq')
- tokens_grad: bfloat16 [32, 512, 768], P('dp', 'seq')
- qkv_weight_grad: float32 [1, 768, 2304], P(None, ('dp', 'seq'))
- qv_bias_grad: float32 [1, 1536], P(None, ('dp', 'seq'))
- out_weight_grad: float32 [1, 768, 768], P(None, ('dp', 'seq'))
- out_bias_grad: float32 [1, 768], P(None, ('dp', 'seq'))
- norm_gain_grad: float32 [1, 768], P(None, ('dp', 'seq'))
- norm_shift_grad: float32 [1, 768], P(None, ('dp', 'seq'))
- up_weight_grad: float32 [1, 768, 3072], P(None, ('dp', 'seq'))
- up_bias_grad: float32 [1, 3072], P(None, ('dp', 'seq'))
- down_weight_grad: float32 [1, 3072, 768], P(None, ('dp', 'seq'))
- down_bias_grad: float32 [1, 768], P(None, ('dp', 'seq'))
- final_gain_grad: float32 [1, 768], P(None, ('dp', 'seq'))
- final_shift_grad: float32 [1, 768], P(None, ('dp', 'seq'))
The draws below stay inside these ranges and needn't reach their ends.
Inputs may be any that keep to these rules, and one draw needn't show every extreme that they name: `lengths`: some sequence is full and some has exactly one eighth of 512 valid tokens.
All inputs are finite; a program needn't handle non-finite values.
Results may differ from the reference program's by a relative error of at most 0.015.
Values may be sent and summed in bfloat16 or wider, within the bound.
A program may use at most 192 MiB of HBM per device.

```python
import jax
import jax.numpy as jnp
from jax import lax

D = 768
HEADS = 12
FF = 3072
HDIM = 64
LAYERS = 1
LEN = 512
SEQS = 32


def draw_lengths(key, part):
    first_key = jax.random.fold_in(key, 11)
    second_key = jax.random.fold_in(key, 12)
    drawn = jax.random.randint(first_key, (SEQS,), LEN // 8, LEN + 1)
    order = jax.random.permutation(second_key, SEQS)
    drawn = drawn.at[order[0]].set(LEN)
    drawn = drawn.at[order[1]].set(LEN // 8)
    return drawn.astype(jnp.int32)


def shard_levels(stream_key, dims, cuts, smallest, largest):
    factor_of, own = 1.0, jax.random.fold_in(stream_key, 6)
    for axis_at, parts in cuts:
        heights = jnp.exp(jax.random.uniform(jax.random.fold_in(own, axis_at), (parts,), jnp.float32, smallest / len(cuts), largest / len(cuts)))
        factor_of = factor_of * jnp.repeat(heights, dims[axis_at] // parts).reshape([-1 if axis == axis_at else 1 for axis in range(len(dims))])
    return factor_of


def normal_values(stream_key, dims, deviation, most, split=(), kind=jnp.bfloat16):
    array = jax.random.normal(stream_key, dims, jnp.float32) * deviation
    if len(split) > 0:
        array = shard_levels(stream_key, dims, split, -0.22, 0.18) * array
    return jnp.clip(array, min=-most, max=most).astype(kind)


def setup_inputs(seed: int = 0) -> dict:
    key_of = jax.random.split(jax.random.key(seed), 16)
    return {
        "tokens": normal_values(key_of[0], (SEQS, LEN, D), 1.0, 6.0, ((0, 8), (1, 4))),
        "cotangent": normal_values(key_of[1], (SEQS, LEN, D), 1.0, 6.0, ((0, 8), (1, 4))),
        "lengths": draw_lengths(jax.random.fold_in(key_of[15], 71), 0),
        "qkv_weight": normal_values(key_of[3], (LAYERS, D, 3 * D), D ** -0.5, 0.21875, ((1, 32),)),
        "qv_bias": normal_values(key_of[4], (LAYERS, 2 * D), 0.5, 3.0, ((1, 32),)),
        "out_weight": normal_values(key_of[5], (LAYERS, D, D), (max(4, D * 8 // LEN)) ** -0.5, 1.75, ((1, 32),)),
        "out_bias": normal_values(key_of[6], (LAYERS, D), 0.5, 3.0, ((1, 32),)),
        "norm_gain": jnp.clip(1.0 + 0.1 * jax.random.normal(key_of[7], (LAYERS, D), jnp.float32), 0.5, 1.5).astype(jnp.bfloat16),
        "norm_shift": normal_values(key_of[8], (LAYERS, D), 0.5, 3.0, ((1, 32),)),
        "up_weight": normal_values(key_of[9], (LAYERS, D, FF), D ** -0.5, 0.21875, ((1, 32),)),
        "up_bias": normal_values(key_of[10], (LAYERS, FF), 0.5, 3.0, ((1, 32),)),
        "down_weight": normal_values(key_of[11], (LAYERS, FF, D), FF ** -0.5, 0.109375, ((1, 32),)),
        "down_bias": normal_values(key_of[12], (LAYERS, D), 0.5, 3.0, ((1, 32),)),
        "final_gain": jnp.clip(1.0 + 0.1 * jax.random.normal(key_of[13], (LAYERS, D), jnp.float32), 0.5, 1.5).astype(jnp.bfloat16),
        "final_shift": normal_values(key_of[14], (LAYERS, D), 0.5, 3.0, ((1, 32),)),
    }


NEG = -1e+30
EPS = 1e-05
HIGH = lax.Precision.HIGHEST

def norm_rows(residual, gain_vec, shift_vec):
    centred = residual - lax.optimization_barrier(jnp.mean(residual, axis=-1, keepdims=True))
    inv_std = lax.rsqrt(lax.optimization_barrier(jnp.mean(centred * centred, axis=-1, keepdims=True)) + EPS)
    normed = centred * inv_std
    return (normed * gain_vec + shift_vec, normed, inv_std)

def norm_back(grad_out, normed, inv_std, gain_vec):
    scaled = grad_out * gain_vec
    return inv_std * (scaled - lax.optimization_barrier(jnp.mean(scaled, axis=-1, keepdims=True)) - normed * lax.optimization_barrier(jnp.mean(scaled * normed, axis=-1, keepdims=True)))

def gelu_exact(value):
    return 0.5 * value * (1.0 + lax.erf(value * 0.7071067811865476))

def gelu_slope(value):
    return 0.5 * (1.0 + lax.erf(value * 0.7071067811865476)) + value * jnp.exp(-0.5 * value * value) * 0.3989422804014327

def head_scores(queries, keys_here, valid):
    scores = jnp.einsum('hqd,hkd->hqk', queries.astype(jnp.float32), keys_here.astype(jnp.float32), precision=HIGH) * HDIM ** (-0.5)
    return jnp.where(valid[None, None, :], scores, NEG)

def attend(queries, keys_here, values, valid):
    scores = head_scores(queries, keys_here, valid)
    row_max = lax.optimization_barrier(jnp.max(scores, axis=-1, keepdims=True))
    log_total = row_max + jnp.log(lax.optimization_barrier(jnp.sum(jnp.exp(scores - row_max), axis=-1, keepdims=True)))
    attn_probs = jnp.exp(scores - log_total).astype(jnp.bfloat16)
    context = jnp.einsum('hqk,hkd->hqd', attn_probs.astype(jnp.float32), values.astype(jnp.float32), precision=HIGH).astype(jnp.bfloat16)
    return (context, log_total)

def attend_back(queries, keys_here, values, context, log_total, d_context, valid):
    scores = head_scores(queries, keys_here, valid)
    attn_probs = jnp.exp(scores - log_total)
    probs_half = attn_probs.astype(jnp.bfloat16).astype(jnp.float32)
    d_ctx32 = d_context.astype(jnp.float32)
    d_values = jnp.einsum('hqk,hqd->hkd', probs_half, d_ctx32, precision=HIGH)
    d_probs = jnp.einsum('hqd,hkd->hqk', d_ctx32, values.astype(jnp.float32), precision=HIGH)
    delta = lax.optimization_barrier(jnp.sum(d_ctx32 * context.astype(jnp.float32), axis=-1, keepdims=True))
    d_scores = (attn_probs * (d_probs - delta) * HDIM ** (-0.5)).astype(jnp.bfloat16).astype(jnp.float32)
    d_queries = jnp.einsum('hqk,hkd->hqd', d_scores, keys_here.astype(jnp.float32), precision=HIGH)
    d_keys = jnp.einsum('hqk,hqd->hkd', d_scores, queries.astype(jnp.float32), precision=HIGH)
    return (d_queries.astype(jnp.bfloat16), d_keys.astype(jnp.bfloat16), d_values.astype(jnp.bfloat16))

def mm(left, right):
    return jnp.dot(left, right, preferred_element_type=jnp.float32)

def one_sequence(seq_tokens, seq_grad, length, params):
    valid = jnp.arange(LEN, dtype=jnp.int32) < length
    hidden = seq_tokens.astype(jnp.float32)
    tapes = []
    for current in range(LAYERS):
        mix_w, mix_b, proj_w, proj_b, gain_one, shift_one, upper_w, upper_b, lower_w, lower_b, gain_two, shift_two = [item[current] for item in params]
        hid_half = hidden.astype(jnp.bfloat16)
        bias_full = jnp.concatenate([mix_b[:D].astype(jnp.float32), jnp.zeros((D,), jnp.float32), mix_b[D:].astype(jnp.float32)])
        mixed = (mm(hid_half, mix_w) + bias_full).astype(jnp.bfloat16)
        heads_view = mixed.reshape(LEN, 3, HEADS, HDIM).transpose(1, 2, 0, 3)
        queries, keys_here, values = (heads_view[0], heads_view[1], heads_view[2])
        context, log_total = attend(queries, keys_here, values, valid)
        context_tok = context.transpose(1, 0, 2).reshape(LEN, D)
        attn_out = mm(context_tok, proj_w) + proj_b.astype(jnp.float32)
        first_norm, normed_one, inv_one = norm_rows(hidden + attn_out, gain_one.astype(jnp.float32), shift_one.astype(jnp.float32))
        first_half = first_norm.astype(jnp.bfloat16)
        pre_act = mm(first_half, upper_w) + upper_b.astype(jnp.float32)
        activated = gelu_exact(pre_act).astype(jnp.bfloat16)
        mlp_out = mm(activated, lower_w) + lower_b.astype(jnp.float32)
        hidden, normed_two, inv_two = norm_rows(first_norm + mlp_out, gain_two.astype(jnp.float32), shift_two.astype(jnp.float32))
        tapes.append((hid_half, queries, keys_here, values, context, log_total, context_tok, normed_one, inv_one, first_half, pre_act, activated, normed_two, inv_two))
    grad = seq_grad.astype(jnp.float32)
    layer_grads = [None] * LAYERS
    for current in reversed(range(LAYERS)):
        mix_w, mix_b, proj_w, proj_b, gain_one, shift_one, upper_w, upper_b, lower_w, lower_b, gain_two, shift_two = [item[current] for item in params]
        hid_half, queries, keys_here, values, context, log_total, context_tok, normed_one, inv_one, first_half, pre_act, activated, normed_two, inv_two = tapes[current]
        d_gain_two = lax.optimization_barrier(jnp.sum(grad * normed_two, axis=0))
        d_shift_two = lax.optimization_barrier(jnp.sum(grad, axis=0))
        d_second = norm_back(grad, normed_two, inv_two, gain_two.astype(jnp.float32))
        d_second_half = d_second.astype(jnp.bfloat16)
        d_lower_b = lax.optimization_barrier(jnp.sum(d_second, axis=0))
        d_lower_w = mm(activated.T, d_second_half)
        d_pre = mm(d_second_half, lower_w.T) * gelu_slope(pre_act)
        d_pre_half = d_pre.astype(jnp.bfloat16)
        d_upper_b = lax.optimization_barrier(jnp.sum(d_pre, axis=0))
        d_upper_w = mm(first_half.T, d_pre_half)
        d_first = d_second + mm(d_pre_half, upper_w.T)
        d_gain_one = lax.optimization_barrier(jnp.sum(d_first * normed_one, axis=0))
        d_shift_one = lax.optimization_barrier(jnp.sum(d_first, axis=0))
        d_resid = norm_back(d_first, normed_one, inv_one, gain_one.astype(jnp.float32))
        d_resid_half = d_resid.astype(jnp.bfloat16)
        d_proj_b = lax.optimization_barrier(jnp.sum(d_resid, axis=0))
        d_proj_w = mm(context_tok.T, d_resid_half)
        d_context = mm(d_resid_half, proj_w.T).astype(jnp.bfloat16)
        d_ctx_heads = d_context.reshape(LEN, HEADS, HDIM).transpose(1, 0, 2)
        d_queries, d_keys, d_values = attend_back(queries, keys_here, values, context, log_total, d_ctx_heads, valid)
        d_mixed = jnp.stack([d_queries, d_keys, d_values]).transpose(2, 0, 1, 3).reshape(LEN, 3 * D)
        col_sums = lax.optimization_barrier(jnp.sum(d_mixed.astype(jnp.float32), axis=0))
        d_mix_b = jnp.concatenate([col_sums[:D], col_sums[2 * D:]])
        d_mix_w = mm(hid_half.T, d_mixed)
        grad = d_resid + mm(d_mixed, mix_w.T)
        layer_grads[current] = (d_mix_w, d_mix_b, d_proj_w, d_proj_b, d_gain_one, d_shift_one, d_upper_w, d_upper_b, d_lower_w, d_lower_b, d_gain_two, d_shift_two)
    stacked = tuple((jnp.stack([layer_grads[current][slot] for current in range(LAYERS)]) for slot in range(12)))
    return (hidden.astype(jnp.bfloat16), grad.astype(jnp.bfloat16), stacked)

def reference(tokens, cotangent, lengths, qkv_weight, qv_bias, out_weight, out_bias, norm_gain, norm_shift, up_weight, up_bias, down_weight, down_bias, final_gain, final_shift):
    params = (qkv_weight, qv_bias, out_weight, out_bias, norm_gain, norm_shift, up_weight, up_bias, down_weight, down_bias, final_gain, final_shift)
    zeros_init = tuple((jnp.zeros(item.shape, jnp.float32) for item in params))

    def step_fn(running, pieces):
        seq_tokens, seq_grad, length = pieces
        seq_out, seq_dx, stacked = one_sequence(seq_tokens, seq_grad, length, params)
        return (tuple((left + right for left, right in zip(running, stacked))), (seq_out, seq_dx))
    totals, (outputs, input_grads) = lax.scan(step_fn, zeros_init, (tokens, cotangent, lengths))
    return (outputs, input_grads, totals[0], totals[1], totals[2], totals[3], totals[4], totals[5], totals[6], totals[7], totals[8], totals[9], totals[10], totals[11])
```

```python
import jax
import jax.numpy as jnp
from jax import lax
from jax.sharding import PartitionSpec as P

HEADS = 12
LAYERS = 1


NEG = -1e30
EPS = 1e-05
SENT = jnp.bfloat16


def norm_rows(residual, gain_vec, shift_vec):
    centred = residual - jnp.mean(residual, axis=-1, keepdims=True)
    inv_std = lax.rsqrt(jnp.mean(centred * centred, axis=-1, keepdims=True) + EPS)
    normed = centred * inv_std
    return (normed * gain_vec + shift_vec, normed, inv_std)


def norm_back(grad_out, normed, inv_std, gain_vec):
    scaled = grad_out * gain_vec
    return inv_std * (
        scaled
        - jnp.mean(scaled, axis=-1, keepdims=True)
        - normed * jnp.mean(scaled * normed, axis=-1, keepdims=True)
    )


def gelu_exact(value):
    return 0.5 * value * (1.0 + lax.erf(value * 0.7071067811865476))


def gelu_slope(value):
    return (
        0.5 * (1.0 + lax.erf(value * 0.7071067811865476))
        + value * jnp.exp(-0.5 * value * value) * 0.3989422804014327
    )


def matmul(left, right):
    return jnp.dot(left, right, preferred_element_type=jnp.float32)


def dot_rows(left, right):
    return lax.dot_general(
        left, right, (((0,), (0,)), ((), ())), preferred_element_type=jnp.float32
    )


def dot_back(left, right):
    return lax.dot_general(
        left, right, (((1,), (1,)), ((), ())), preferred_element_type=jnp.float32
    )


def per_device(
    tokens,
    cotangent,
    lengths,
    qkv_weight,
    qv_bias,
    out_weight,
    out_bias,
    norm_gain,
    norm_shift,
    up_weight,
    up_bias,
    down_weight,
    down_bias,
    final_gain,
    final_shift,
):
    groups = lax.axis_size("seq")
    seq_here, tok_here, model_width = tokens.shape
    head_count = HEADS
    head_dim = model_width // head_count
    row_count = seq_here * tok_here
    key_count = tok_here * groups
    pair_count = seq_here * head_count // groups
    block_rows = min(512, key_count)
    block_count = key_count // block_rows
    score_scale = head_dim ** (-0.5)
    pair_ids = lax.axis_index("seq") * pair_count + jnp.arange(pair_count, dtype=jnp.int32)
    owners = pair_ids // head_count
    picked = owners[:, None] == jnp.arange(seq_here, dtype=jnp.int32)[None, :]
    pair_len = jnp.sum(jnp.where(picked, lengths[None, :], 0), axis=1)
    valid = jnp.arange(key_count, dtype=jnp.int32)[None, :] < pair_len[:, None]

    def to_heads(table, parts):
        shaped = table.reshape(seq_here, tok_here, parts, head_count, head_dim).transpose(
            0, 3, 1, 2, 4
        )
        return shaped.reshape(seq_here * head_count, tok_here, parts * head_dim)

    def from_heads(table, parts):
        shaped = table.reshape(seq_here, head_count, tok_here, parts, head_dim).transpose(
            0, 2, 3, 1, 4
        )
        return shaped.reshape(row_count, parts * model_width)

    def to_blocks(table):
        return table.reshape(pair_count, block_count, block_rows, table.shape[-1]).transpose(
            1, 0, 2, 3
        )

    def from_blocks(table):
        return table.transpose(1, 0, 2, 3).reshape(pair_count, key_count, table.shape[-1])

    def block_scores(q_block, keys_here):
        scores = (
            jnp.einsum("pqd,pkd->pqk", q_block, keys_here, preferred_element_type=jnp.float32)
            * score_scale
        )
        return jnp.where(valid[:, None, :], scores, NEG)

    hidden = tokens.reshape(row_count, model_width).astype(jnp.float32)
    kept_params = []
    current = 0
    params = (
        lax.all_gather(qkv_weight[current], ("dp", "seq"), axis=0, tiled=True),
        lax.all_gather(qv_bias[current], ("dp", "seq"), axis=0, tiled=True),
        lax.all_gather(out_weight[current], ("dp", "seq"), axis=0, tiled=True),
        lax.all_gather(out_bias[current], ("dp", "seq"), axis=0, tiled=True),
        lax.all_gather(norm_gain[current], ("dp", "seq"), axis=0, tiled=True),
        lax.all_gather(norm_shift[current], ("dp", "seq"), axis=0, tiled=True),
        lax.all_gather(up_weight[current], ("dp", "seq"), axis=0, tiled=True),
        lax.all_gather(up_bias[current], ("dp", "seq"), axis=0, tiled=True),
        lax.all_gather(down_weight[current], ("dp", "seq"), axis=0, tiled=True),
        lax.all_gather(down_bias[current], ("dp", "seq"), axis=0, tiled=True),
        lax.all_gather(final_gain[current], ("dp", "seq"), axis=0, tiled=True),
        lax.all_gather(final_shift[current], ("dp", "seq"), axis=0, tiled=True),
    )
    kept_params.append(None)
    (
        mix_w,
        mix_b,
        proj_w,
        proj_b,
        gain_one,
        shift_one,
        upper_w,
        upper_b,
        lower_w,
        lower_b,
        gain_two,
        shift_two,
    ) = params
    hid_half = hidden.astype(jnp.bfloat16)
    bias_full = jnp.concatenate(
        [
            mix_b[:model_width].astype(jnp.float32),
            jnp.zeros((model_width,), jnp.float32),
            mix_b[model_width:].astype(jnp.float32),
        ]
    )
    mixed = (matmul(hid_half, mix_w) + bias_full).astype(jnp.bfloat16)
    by_heads = lax.all_to_all(to_heads(mixed, 3), "seq", split_axis=0, concat_axis=1, tiled=True)
    queries = by_heads[..., :head_dim]
    keys_here = by_heads[..., head_dim : 2 * head_dim]
    values = by_heads[..., 2 * head_dim :]

    def one_block(q_block):
        scores = block_scores(q_block, keys_here)
        row_max = jnp.max(scores, axis=-1, keepdims=True)
        log_total = row_max + jnp.log(jnp.sum(jnp.exp(scores - row_max), axis=-1, keepdims=True))
        attn_probs = jnp.exp(scores - log_total).astype(jnp.bfloat16)
        context = jnp.einsum(
            "pqk,pkd->pqd", attn_probs, values, preferred_element_type=jnp.float32
        ).astype(jnp.bfloat16)
        return (context, log_total[..., 0])

    context, log_total = lax.map(one_block, to_blocks(queries))
    context, log_total = (
        from_blocks(context),
        log_total.transpose(1, 0, 2).reshape(pair_count, key_count),
    )
    context_tok = from_heads(
        lax.all_to_all(context, "seq", split_axis=1, concat_axis=0, tiled=True), 1
    )
    attn_out = matmul(context_tok, proj_w) + proj_b.astype(jnp.float32)
    first_norm, normed_one, inv_one = norm_rows(
        hidden + attn_out, gain_one.astype(jnp.float32), shift_one.astype(jnp.float32)
    )
    first_half = first_norm.astype(jnp.bfloat16)
    pre_act = matmul(first_half, upper_w) + upper_b.astype(jnp.float32)
    activated = gelu_exact(pre_act).astype(jnp.bfloat16)
    mlp_out = matmul(activated, lower_w) + lower_b.astype(jnp.float32)
    hidden, normed_two, inv_two = norm_rows(
        first_norm + mlp_out, gain_two.astype(jnp.float32), shift_two.astype(jnp.float32)
    )
    tapes = [
        (
            hid_half,
            queries,
            keys_here,
            values,
            context,
            log_total,
            context_tok,
            normed_one,
            inv_one,
            first_half,
            pre_act,
            activated,
            normed_two,
            inv_two,
        )
    ]
    output = hidden.astype(jnp.bfloat16).reshape(tokens.shape)
    grad = cotangent.reshape(row_count, model_width).astype(jnp.float32)
    shares = [None] * LAYERS
    for current in reversed(range(LAYERS)):
        params = (
            lax.all_gather(qkv_weight[current], ("dp", "seq"), axis=0, tiled=True),
            lax.all_gather(qv_bias[current], ("dp", "seq"), axis=0, tiled=True),
            lax.all_gather(out_weight[current], ("dp", "seq"), axis=0, tiled=True),
            lax.all_gather(out_bias[current], ("dp", "seq"), axis=0, tiled=True),
            lax.all_gather(norm_gain[current], ("dp", "seq"), axis=0, tiled=True),
            lax.all_gather(norm_shift[current], ("dp", "seq"), axis=0, tiled=True),
            lax.all_gather(up_weight[current], ("dp", "seq"), axis=0, tiled=True),
            lax.all_gather(up_bias[current], ("dp", "seq"), axis=0, tiled=True),
            lax.all_gather(down_weight[current], ("dp", "seq"), axis=0, tiled=True),
            lax.all_gather(down_bias[current], ("dp", "seq"), axis=0, tiled=True),
            lax.all_gather(final_gain[current], ("dp", "seq"), axis=0, tiled=True),
            lax.all_gather(final_shift[current], ("dp", "seq"), axis=0, tiled=True),
        )
        (
            mix_w,
            mix_b,
            proj_w,
            proj_b,
            gain_one,
            shift_one,
            upper_w,
            upper_b,
            lower_w,
            lower_b,
            gain_two,
            shift_two,
        ) = params
        (
            hid_half,
            queries,
            keys_here,
            values,
            context,
            log_total,
            context_tok,
            normed_one,
            inv_one,
            first_half,
            pre_act,
            activated,
            normed_two,
            inv_two,
        ) = tapes[current]
        d_gain_two = jnp.sum(grad * normed_two, axis=0)
        d_shift_two = jnp.sum(grad, axis=0)
        d_second = norm_back(grad, normed_two, inv_two, gain_two.astype(jnp.float32))
        d_second_half = d_second.astype(jnp.bfloat16)
        d_lower_b = jnp.sum(d_second, axis=0)
        d_lower_w = dot_rows(activated, d_second_half)
        d_pre = dot_back(d_second_half, lower_w) * gelu_slope(pre_act)
        d_pre_half = d_pre.astype(jnp.bfloat16)
        d_upper_b = jnp.sum(d_pre, axis=0)
        d_upper_w = dot_rows(first_half, d_pre_half)
        d_first = d_second + dot_back(d_pre_half, upper_w)
        d_gain_one = jnp.sum(d_first * normed_one, axis=0)
        d_shift_one = jnp.sum(d_first, axis=0)
        d_resid = norm_back(d_first, normed_one, inv_one, gain_one.astype(jnp.float32))
        d_resid_half = d_resid.astype(jnp.bfloat16)
        d_proj_b = jnp.sum(d_resid, axis=0)
        d_proj_w = dot_rows(context_tok, d_resid_half)
        d_context = dot_back(d_resid_half, proj_w).astype(jnp.bfloat16)
        d_ctx_heads = lax.all_to_all(
            to_heads(d_context, 1), "seq", split_axis=0, concat_axis=1, tiled=True
        )
        totals_blocks = log_total.reshape(pair_count, block_count, block_rows).transpose(1, 0, 2)

        def attend_one_block(running, pieces):
            q_block, o_block, do_block, lse_block = pieces
            scores = block_scores(q_block, keys_here)
            attn_probs = jnp.exp(scores - lse_block[..., None])
            probs_half = attn_probs.astype(jnp.bfloat16)
            d_values = running[1] + jnp.einsum(
                "pqk,pqd->pkd", probs_half, do_block, preferred_element_type=jnp.float32
            )
            d_probs = jnp.einsum(
                "pqd,pkd->pqk", do_block, values, preferred_element_type=jnp.float32
            )
            delta = jnp.sum(
                do_block.astype(jnp.float32) * o_block.astype(jnp.float32), axis=-1, keepdims=True
            )
            d_scores = (attn_probs * (d_probs - delta) * score_scale).astype(jnp.bfloat16)
            d_queries = jnp.einsum(
                "pqk,pkd->pqd", d_scores, keys_here, preferred_element_type=jnp.float32
            ).astype(jnp.bfloat16)
            d_keys = running[0] + jnp.einsum(
                "pqk,pqd->pkd", d_scores, q_block, preferred_element_type=jnp.float32
            )
            return ((d_keys, d_values), d_queries)

        zero_init = jnp.zeros((pair_count, key_count, head_dim), jnp.float32)
        (d_keys, d_values), d_queries = lax.scan(
            attend_one_block,
            (zero_init, zero_init),
            (to_blocks(queries), to_blocks(context), to_blocks(d_ctx_heads), totals_blocks),
        )
        d_mixed_heads = jnp.concatenate(
            [from_blocks(d_queries), d_keys.astype(jnp.bfloat16), d_values.astype(jnp.bfloat16)],
            axis=-1,
        )
        d_mixed = from_heads(
            lax.all_to_all(d_mixed_heads, "seq", split_axis=1, concat_axis=0, tiled=True), 3
        )
        col_sums = jnp.sum(d_mixed.astype(jnp.float32), axis=0)
        d_mix_b = jnp.concatenate([col_sums[:model_width], col_sums[2 * model_width :]])
        d_mix_w = dot_rows(hid_half, d_mixed)
        grad = d_resid + dot_back(d_mixed, mix_w)
        partials = (
            d_mix_w,
            d_mix_b,
            d_proj_w,
            d_proj_b,
            d_gain_one,
            d_shift_one,
            d_upper_w,
            d_upper_b,
            d_lower_w,
            d_lower_b,
            d_gain_two,
            d_shift_two,
        )
        flats = tuple((item.reshape(-1) for item in partials))
        summed = (
            lax.psum_scatter(flats[0], ("dp", "seq"), scatter_dimension=0, tiled=True),
            lax.psum_scatter(flats[1], ("dp", "seq"), scatter_dimension=0, tiled=True),
            lax.psum_scatter(flats[2], ("dp", "seq"), scatter_dimension=0, tiled=True),
            lax.psum_scatter(flats[3], ("dp", "seq"), scatter_dimension=0, tiled=True),
            lax.psum_scatter(flats[4], ("dp", "seq"), scatter_dimension=0, tiled=True),
            lax.psum_scatter(flats[5], ("dp", "seq"), scatter_dimension=0, tiled=True),
            lax.psum_scatter(flats[6], ("dp", "seq"), scatter_dimension=0, tiled=True),
            lax.psum_scatter(flats[7], ("dp", "seq"), scatter_dimension=0, tiled=True),
            lax.psum_scatter(flats[8], ("dp", "seq"), scatter_dimension=0, tiled=True),
            lax.psum_scatter(flats[9], ("dp", "seq"), scatter_dimension=0, tiled=True),
            lax.psum_scatter(flats[10], ("dp", "seq"), scatter_dimension=0, tiled=True),
            lax.psum_scatter(flats[11], ("dp", "seq"), scatter_dimension=0, tiled=True),
        )
        shares[current] = tuple(
            (piece.reshape((-1,) + whole.shape[1:]) for piece, whole in zip(summed, partials))
        )
    input_grad = grad.astype(jnp.bfloat16).reshape(tokens.shape)
    stacked = tuple((jnp.stack([shares[0][slot]]) for slot in range(12)))
    return (output, input_grad) + stacked


def split_cols(table, widths):
    pieces, start = [], 0
    for width in widths:
        pieces.append(table[..., start : start + width])
        start += width
    return pieces


def gather_rows(piece):
    return lax.all_gather(
        lax.all_gather(piece, "seq", axis=0, tiled=True), "dp", axis=0, tiled=True
    )


def scatter_rows(whole):
    part = lax.psum_scatter(
        whole.reshape(-1), ("dp", "seq"), scatter_dimension=0, tiled=True
    )
    return part.astype(jnp.float32).reshape((-1,) + whole.shape[1:])


def per_sequence(
    tokens,
    cotangent,
    lengths,
    qkv_weight,
    qv_bias,
    out_weight,
    out_bias,
    norm_gain,
    norm_shift,
    up_weight,
    up_bias,
    down_weight,
    down_bias,
    final_gain,
    final_shift,
):
    groups = lax.axis_size("seq")
    ranks = lax.axis_size("dp") * groups
    seq_here, tok_here, model_width = tokens.shape
    own = seq_here // groups
    key_count = tok_here * groups
    head_dim = model_width // HEADS
    row_count = own * key_count
    score_scale = head_dim ** (-0.5)

    def to_sequences(table):
        return lax.all_to_all(table, "seq", split_axis=0, concat_axis=1, tiled=True)

    def to_tokens(table):
        return lax.all_to_all(
            table.reshape(own, key_count, model_width),
            "seq",
            split_axis=1,
            concat_axis=0,
            tiled=True,
        )

    def heads_of(table):
        return table.reshape(own, key_count, HEADS, head_dim).transpose(0, 2, 1, 3)

    def flat_of(table):
        return table.transpose(0, 2, 1, 3).reshape(row_count, model_width)

    own_len = lax.dynamic_slice_in_dim(lengths, lax.axis_index("seq") * own, own, axis=0)
    valid = jnp.arange(key_count, dtype=jnp.int32)[None, :] < own_len[:, None]

    smalls = (
        qv_bias[0],
        out_bias[0],
        norm_gain[0],
        norm_shift[0],
        up_bias[0],
        down_bias[0],
        final_gain[0],
        final_shift[0],
    )
    widths = [item.shape[0] for item in smalls]
    hid_half = to_sequences(tokens).reshape(row_count, model_width)
    small_all = lax.all_gather(
        jnp.concatenate(smalls), ("dp", "seq"), axis=0, tiled=True
    ).reshape(ranks, -1)
    mix_w = gather_rows(qkv_weight[0])
    proj_w = gather_rows(out_weight[0])
    upper_w = gather_rows(up_weight[0])
    lower_w = gather_rows(down_weight[0])
    mix_b, proj_b, gain_one, shift_one, upper_b, lower_b, gain_two, shift_two = [
        item.reshape(-1).astype(jnp.float32) for item in split_cols(small_all, widths)
    ]
    grad = to_sequences(cotangent).reshape(row_count, model_width).astype(jnp.float32)

    hidden = hid_half.astype(jnp.float32)
    bias_full = jnp.concatenate(
        [mix_b[:model_width], jnp.zeros((model_width,), jnp.float32), mix_b[model_width:]]
    )
    mixed = (matmul(hid_half, mix_w) + bias_full).astype(jnp.bfloat16)
    queries = heads_of(mixed[:, :model_width])
    keys_here = heads_of(mixed[:, model_width : 2 * model_width])
    values = heads_of(mixed[:, 2 * model_width :])
    scores = (
        jnp.einsum("shqd,shkd->shqk", queries, keys_here, preferred_element_type=jnp.float32)
        * score_scale
    )
    scores = jnp.where(valid[:, None, None, :], scores, NEG)
    row_max = jnp.max(scores, axis=-1, keepdims=True)
    log_total = row_max + jnp.log(jnp.sum(jnp.exp(scores - row_max), axis=-1, keepdims=True))
    attn_probs = jnp.exp(scores - log_total)
    probs_half = attn_probs.astype(jnp.bfloat16)
    context = jnp.einsum(
        "shqk,shkd->shqd", probs_half, values, preferred_element_type=jnp.float32
    ).astype(jnp.bfloat16)
    context_tok = flat_of(context)
    first_norm, normed_one, inv_one = norm_rows(
        hidden + matmul(context_tok, proj_w) + proj_b, gain_one, shift_one
    )
    first_half = first_norm.astype(jnp.bfloat16)
    pre_act = matmul(first_half, upper_w) + upper_b
    activated = gelu_exact(pre_act).astype(jnp.bfloat16)
    last, normed_two, inv_two = norm_rows(
        first_norm + matmul(activated, lower_w) + lower_b, gain_two, shift_two
    )
    output = to_tokens(last.astype(jnp.bfloat16))

    d_gain_two = jnp.sum(grad * normed_two, axis=0)
    d_shift_two = jnp.sum(grad, axis=0)
    d_second = norm_back(grad, normed_two, inv_two, gain_two)
    d_second_half = d_second.astype(jnp.bfloat16)
    d_lower_b = jnp.sum(d_second, axis=0)
    lower_part, d_second_half = lax.optimization_barrier(
        (dot_rows(activated, d_second_half).astype(SENT), d_second_half)
    )
    d_lower_w = scatter_rows(lower_part)
    d_pre = dot_back(d_second_half, lower_w) * gelu_slope(pre_act)
    d_pre_half = d_pre.astype(jnp.bfloat16)
    d_upper_b = jnp.sum(d_pre, axis=0)
    upper_part, d_pre_half = lax.optimization_barrier(
        (dot_rows(first_half, d_pre_half).astype(SENT), d_pre_half)
    )
    d_upper_w = scatter_rows(upper_part)
    d_first = d_second + dot_back(d_pre_half, upper_w)
    d_gain_one = jnp.sum(d_first * normed_one, axis=0)
    d_shift_one = jnp.sum(d_first, axis=0)
    d_resid = norm_back(d_first, normed_one, inv_one, gain_one)
    d_resid_half = d_resid.astype(jnp.bfloat16)
    d_proj_b = jnp.sum(d_resid, axis=0)
    proj_part, d_resid_half = lax.optimization_barrier(
        (dot_rows(context_tok, d_resid_half).astype(SENT), d_resid_half)
    )
    d_proj_w = scatter_rows(proj_part)
    d_ctx_tok = dot_back(d_resid_half, proj_w).astype(jnp.bfloat16)
    d_ctx = heads_of(d_ctx_tok)
    d_values = jnp.einsum(
        "shqk,shqd->shkd", probs_half, d_ctx, preferred_element_type=jnp.float32
    ).astype(jnp.bfloat16)
    d_probs = jnp.einsum("shqd,shkd->shqk", d_ctx, values, preferred_element_type=jnp.float32)
    delta = jnp.sum(
        d_ctx.astype(jnp.float32) * context.astype(jnp.float32), axis=-1, keepdims=True
    )
    d_scores = (attn_probs * (d_probs - delta) * score_scale).astype(jnp.bfloat16)
    d_queries = jnp.einsum(
        "shqk,shkd->shqd", d_scores, keys_here, preferred_element_type=jnp.float32
    ).astype(jnp.bfloat16)
    d_keys = jnp.einsum(
        "shqk,shqd->shkd", d_scores, queries, preferred_element_type=jnp.float32
    ).astype(jnp.bfloat16)
    d_mixed = jnp.concatenate(
        [flat_of(d_queries), flat_of(d_keys), flat_of(d_values)], axis=-1
    )
    col_sums = jnp.sum(d_mixed.astype(jnp.float32), axis=0)
    d_mix_b = jnp.concatenate([col_sums[:model_width], col_sums[2 * model_width :]])
    small_grads = jnp.concatenate(
        [
            item.reshape(ranks, -1)
            for item in (
                d_mix_b,
                d_proj_b,
                d_gain_one,
                d_shift_one,
                d_upper_b,
                d_lower_b,
                d_gain_two,
                d_shift_two,
            )
        ],
        axis=1,
    )
    d_mix_w = scatter_rows(dot_rows(hid_half, d_mixed).astype(SENT))
    (
        s_mix_b,
        s_proj_b,
        s_gain_one,
        s_shift_one,
        s_upper_b,
        s_lower_b,
        s_gain_two,
        s_shift_two,
    ) = split_cols(scatter_rows(small_grads)[0], widths)
    input_grad = to_tokens((d_resid + dot_back(d_mixed, mix_w)).astype(jnp.bfloat16))
    shares = (
        d_mix_w,
        s_mix_b,
        d_proj_w,
        s_proj_b,
        s_gain_one,
        s_shift_one,
        d_upper_w,
        s_upper_b,
        d_lower_w,
        s_lower_b,
        s_gain_two,
        s_shift_two,
    )
    return (output, input_grad) + tuple((item[None] for item in shares))


def choose(*args):
    if args[0].shape[0] % lax.axis_size("seq") == 0:
        return per_sequence(*args)
    return per_device(*args)


def solution(mesh):
    placed = (
        P("dp", "seq", None),
        P("dp", "seq", None),
        P("dp"),
        P(None, ("dp", "seq"), None),
        P(None, ("dp", "seq")),
        P(None, ("dp", "seq"), None),
        P(None, ("dp", "seq")),
        P(None, ("dp", "seq")),
        P(None, ("dp", "seq")),
        P(None, ("dp", "seq"), None),
        P(None, ("dp", "seq")),
        P(None, ("dp", "seq"), None),
        P(None, ("dp", "seq")),
        P(None, ("dp", "seq")),
        P(None, ("dp", "seq")),
    )
    return jax.shard_map(
        choose,
        mesh=mesh,
        in_specs=placed,
        out_specs=(
            P("dp", "seq", None),
            P("dp", "seq", None),
            P(None, ("dp", "seq"), None),
            P(None, ("dp", "seq")),
            P(None, ("dp", "seq"), None),
            P(None, ("dp", "seq")),
            P(None, ("dp", "seq")),
            P(None, ("dp", "seq")),
            P(None, ("dp", "seq"), None),
            P(None, ("dp", "seq")),
            P(None, ("dp", "seq"), None),
            P(None, ("dp", "seq")),
            P(None, ("dp", "seq")),
            P(None, ("dp", "seq")),
        ),
        check_vma=False,
    )
```
